32 devices in a mesh: row: 4 (over x, core), col: 8 (over z, y).
Axes of the slice: x: 2, y: 2, z: 4, core: 2. Of those that a mesh axis runs over, the one named last changes fastest.
Arguments:
- vectors: float32 [16, 4096], P(None, ('row', 'col')), may hold values from -12 to 12, as said below
- diag_energy: float32 [4096], P(('row', 'col')), may hold values from 0.5 to 4
- blocks: float32 [4, 192, 128, 128], P('row', 'col'), may hold values from -0.078125 to 0.078125
- block_row: int32 [4, 192], P('row', 'col'), may hold values from 0 to 7
- block_col: int32 [4, 192], P('row', 'col'), may hold values from 0 to 3
Outputs:
- image: float32 [16, 4096], P(None, ('row', 'col'))
- resid: float32 [16, 4096], P(None, ('row', 'col'))
The draws below stay inside these ranges and needn't reach their ends.
Inputs may be any that keep to these rules, and one draw needn't show every extreme that they name: `vectors`: each row of X holds independent entries; the Gram matrix X X^T is positive definite.
All inputs are finite; a program needn't handle non-finite values.
Results may differ from the reference program's by a relative error of at most 0.0003.
Values sent between devices are 32-bit elements; how exact they have to be, the bound alone decides.
A program may use at most 64 MiB of HBM per device.

```python
import math
import jax
import jax.numpy as jnp
from jax import lax

K = 16
BLK = 128
BPT = 24
SHARD = 128
NDIM = 4096
RB = 8
CB = 4
N_ROW = 4
N_COL = 8


def draw_vectors(key, part):
    first_key = jax.random.fold_in(jax.random.fold_in(key, 11), 0)
    position = jnp.arange(NDIM).astype(jnp.float32)
    scale = jnp.exp(math.log(3.0) * position / NDIM)
    values = jax.random.normal(first_key, (K, NDIM), jnp.float32) * scale[None, :]
    return jnp.clip(values, -12.0, 12.0).astype(jnp.float32)


def set_ends(array, own_key, low, largest):
    longest = array.shape.index(max(array.shape))
    spots = []
    for shift in (0, 1):
        where = [jax.random.randint(jax.random.fold_in(own_key, axis), (), 0, length) for axis, length in enumerate(array.shape)]
        where[longest] = (where[longest] + shift) % array.shape[longest]
        spots.append(tuple(where))
    return array.at[spots[0]].set(low).at[spots[1]].set(largest)


def level_of(rng, extent, cuts, smallest, top_value):
    factor_of, own = 1.0, jax.random.fold_in(rng, 6)
    for axis_at, parts in cuts:
        heights = jnp.exp(jax.random.uniform(jax.random.fold_in(own, axis_at), (parts,), jnp.float32, smallest / len(cuts), top_value / len(cuts)))
        factor_of = factor_of * jnp.repeat(heights, extent[axis_at] // parts).reshape([-1 if axis == axis_at else 1 for axis in range(len(extent))])
    return factor_of


def gaussian(key, dims, width, most, shards=(), dtype=jnp.bfloat16):
    level = level_of(key, dims, shards, -0.22, 0.18) if shards else 1.0
    result = jax.random.normal(key, dims, jnp.float32) * width * level
    return jnp.minimum(jnp.maximum(result, -most), most).astype(dtype)


def setup_inputs(seed: int = 0) -> dict:
    splits = jax.random.split(jax.random.key(seed), 6)
    vectors = draw_vectors(jax.random.fold_in(splits[5], 71), 0)
    diag_energy = jnp.clip(jnp.exp(math.log(4.0) - 2.0794415 * jax.random.uniform(splits[1], (NDIM,), jnp.float32) ** level_of(splits[1], (NDIM,), ((0, 32),), -0.2, 0.2)), 0.5, 4.0)
    blocks = gaussian(splits[2], (N_ROW, N_COL * BPT, BLK, BLK), (2 * BPT * BLK * BLK // SHARD) ** -0.5, 0.078125, ((0, 4), (1, 8)), jnp.float32)
    block_row = set_ends(jax.random.randint(splits[3], (N_ROW, N_COL * BPT), 0, RB), jax.random.fold_in(splits[3], 1), 0, RB - 1).astype(jnp.int32)
    block_col = set_ends(jax.random.randint(splits[4], (N_ROW, N_COL * BPT), 0, CB), jax.random.fold_in(splits[4], 1), 0, CB - 1).astype(jnp.int32)
    return {"vectors": vectors, "diag_energy": diag_energy, "blocks": blocks, "block_row": block_row, "block_col": block_col}


def solve_metric(metric, gram):
    highest = lax.Precision.HIGHEST
    order = metric.shape[0]
    index = jnp.arange(order).astype(jnp.int32)
    factor = jnp.zeros_like(metric)
    for column in range(order):
        onehot = (index == column).astype(jnp.float32)
        rest = metric[:, column] - jnp.dot(factor, factor[column, :], precision=highest)
        pivot = jnp.sqrt(rest[column])
        values = jnp.where(index >= column, rest / pivot, 0.0)
        factor = factor + values[:, None] * onehot[None, :]
    inner = jnp.zeros_like(gram)
    for line in range(order):
        onehot = (index == line).astype(jnp.float32)
        value = (gram[line, :] - jnp.dot(factor[line, :], inner, precision=highest)) / factor[line, line]
        inner = inner + onehot[:, None] * value[None, :]
    solved = jnp.zeros_like(gram)
    for line in range(order - 1, -1, -1):
        onehot = (index == line).astype(jnp.float32)
        value = (inner[line, :] - jnp.dot(factor[:, line], solved, precision=highest)) / factor[line, line]
        solved = solved + onehot[:, None] * value[None, :]
    return solved

def reference(vectors, diag_energy, blocks, block_row, block_col):
    highest = lax.Precision.HIGHEST
    row_blocks = SHARD * N_COL // BLK
    col_blocks = SHARD * N_ROW // BLK
    xvec = vectors
    xrow = xvec.reshape(K, N_ROW, row_blocks, BLK).transpose(1, 0, 2, 3)
    xcol = xvec.reshape(K, N_ROW, N_COL, SHARD).transpose(0, 2, 1, 3).reshape(K, N_COL, col_blocks, BLK)
    tile_col = (jnp.arange(N_COL * BPT) // BPT).astype(jnp.int32)
    row_iota = jnp.arange(row_blocks).astype(jnp.int32)
    col_iota = jnp.arange(N_COL * col_blocks).astype(jnp.int32)

    def one_row(carry, inputs):
        tiles, rows_here, cols_here, xr_here = inputs
        picked = xcol[:, tile_col, cols_here]
        terms = jnp.einsum('bij,kbj->kbi', tiles, picked, precision=highest)
        onehot = (rows_here[:, None] == row_iota[None, :]).astype(jnp.float32)
        part_one = jnp.einsum('kbi,br->kri', terms, onehot, precision=highest)
        picked_two = xr_here[:, rows_here]
        terms_two = jnp.einsum('bij,kbi->kbj', tiles, picked_two, precision=highest)
        onehot_two = ((tile_col * col_blocks + cols_here)[:, None] == col_iota[None, :]).astype(jnp.float32)
        part_two = jnp.einsum('kbj,bq->kqj', terms_two, onehot_two, precision=highest)
        return (carry + part_two, part_one)
    start = jnp.zeros((K, N_COL * col_blocks, BLK), jnp.float32)
    col_sum, row_parts = lax.scan(one_row, start, (blocks, block_row, block_col, xrow))
    first = row_parts.transpose(1, 0, 2, 3).reshape(K, NDIM)
    second = col_sum.reshape(K, N_COL, N_ROW, SHARD).transpose(0, 2, 1, 3).reshape(K, NDIM)
    image = first + second + diag_energy[None, :] * xvec
    gram = jnp.dot(xvec, image.T, precision=highest, preferred_element_type=jnp.float32)
    metric = jnp.dot(xvec, xvec.T, precision=highest, preferred_element_type=jnp.float32)
    coef = solve_metric(metric, gram)
    resid = image - jnp.dot(coef.T, xvec, precision=highest, preferred_element_type=jnp.float32)
    return (image, resid)
```

```python
import functools

import jax
import jax.numpy as jnp
from jax import lax
from jax.experimental import pallas as pl
from jax.experimental.pallas import tpu as pltpu
from jax.sharding import PartitionSpec as P

BLK = 128
F32 = jnp.float32
BF16 = jnp.bfloat16
MESH = pl.DeviceIdType.MESH


def halves(x):
    high = x.astype(BF16)
    return high, (x - high.astype(F32)).astype(BF16)


def dot_nt(a, b):
    return lax.dot_general(a, b, (((1,), (1,)), ((), ())), preferred_element_type=F32)


def dot_nn(a, b):
    return lax.dot_general(a, b, (((1,), (0,)), ((), ())), preferred_element_type=F32)


def kernel(
    n_row, n_col,
    x_ref, diag_ref, rows_ref, cols_ref, blocks_ref,
    image_ref, resid_ref,
    tiles, split, col_x, row_x, col_lhs, row_lhs,
    met_out, met_in, p1_out, p1_in, p2_out, p2_in, g1_out, g1_in, g2_out, g2_in,
    tile_sem, cx_s, cx_r, rx_s, rx_r, m_s, m_r, p1_s, p1_r, p2_s, p2_r, g1_s, g1_r, g2_s, g2_r,
):
    count = x_ref.shape[0]
    n_blk = tiles.shape[0]
    my_row = lax.axis_index("row")
    my_col = lax.axis_index("col")

    def fan(axis, size, me, source, target, send, recv):
        copies = []
        for d in range(1, size):
            peer = lax.rem(me + d, size)
            copies.append(
                pltpu.make_async_remote_copy(
                    src_ref=source(peer), dst_ref=target(d), send_sem=send.at[d],
                    recv_sem=recv.at[d], device_id={axis: peer}, device_id_type=MESH,
                )
            )
        for copy in copies:
            copy.start()
        return copies

    fan_row = functools.partial(fan, "row", n_row, my_row)
    fan_col = functools.partial(fan, "col", n_col, my_col)

    load = pltpu.make_async_copy(blocks_ref.at[0], tiles, tile_sem)
    load.start()

    barrier = pltpu.get_barrier_semaphore()
    for d in range(1, n_col):
        pl.semaphore_signal(
            barrier, inc=1, device_id={"col": lax.rem(my_col + d, n_col)}, device_id_type=MESH
        )
    for d in range(1, n_row):
        pl.semaphore_signal(
            barrier, inc=1, device_id={"row": lax.rem(my_row + d, n_row)}, device_id_type=MESH
        )
    pl.semaphore_wait(barrier, n_row + n_col - 2)

    row_copies = fan_col(lambda peer: x_ref, lambda d: row_x.at[my_col], rx_s, rx_r)
    col_copies = fan_row(lambda peer: x_ref, lambda d: col_x.at[my_row], cx_s, cx_r)
    x_own = x_ref[...]
    row_x[my_col] = x_own
    col_x[my_row] = x_own

    load.wait()
    for b in range(n_blk):
        high, low = halves(tiles[b])
        split[b] = jnp.concatenate([high, low], axis=1)

    for copy in col_copies:
        copy.wait()
    zero = jnp.zeros((count, BLK), BF16)
    for q in range(n_row):
        high, low = halves(col_x[q])
        col_lhs[q] = jnp.concatenate(
            [jnp.concatenate([high, high], axis=1), jnp.concatenate([low, zero], axis=1)], axis=0
        )
    for copy in row_copies:
        copy.wait()
    row_two = []
    for r in range(n_col):
        high, low = halves(row_x[r])
        both = jnp.concatenate([high, low], axis=0)
        row_lhs[r] = both
        row_two.append(both)

    def fold(o):
        return o[:count, :count] + o[count:, :count] + o[:count, count:]

    x_wide = jnp.concatenate(row_two, axis=1)
    metric_part = fold(dot_nt(x_wide, x_wide))
    met_out[...] = jnp.concatenate(
        [metric_part, jnp.zeros((count, BLK - count), F32)], axis=1
    )
    met_copies = fan_row(lambda peer: met_out, lambda d: met_in.at[d], m_s, m_r)

    part_one = [jnp.zeros((count, BLK), F32) for _ in range(n_col)]
    for b in range(n_blk):
        o = dot_nt(col_lhs[cols_ref[0, b]], split[b])
        term = o[:count] + o[count:]
        place = rows_ref[0, b]
        for r in range(n_col):
            part_one[r] = part_one[r] + (place == r).astype(F32) * term
    for r in range(n_col):
        p1_out[r] = part_one[r]
    p1_copies = fan_col(lambda peer: p1_out.at[peer], lambda d: p1_in.at[d], p1_s, p1_r)

    own_diag = diag_ref[...] * x_own
    p_two = [jnp.concatenate(halves(p), axis=0) for p in part_one]
    x_two = jnp.concatenate(halves(x_own), axis=0)
    d_two = jnp.concatenate(halves(own_diag), axis=0)
    gram_part = fold(
        dot_nt(
            jnp.concatenate(row_two + p_two + [x_two], axis=1),
            jnp.concatenate(p_two + row_two + [d_two], axis=1),
        )
    )
    per = BLK // count
    groups = count // 8
    lane = lax.broadcasted_iota(jnp.int32, (count, BLK), 1)
    sub = lax.broadcasted_iota(jnp.int32, (count, BLK), 0)
    keep = (lane // count) == (sub % per)
    spread = jnp.where(keep, jnp.concatenate([gram_part] * per, axis=1), 0.0)
    g1_out[...] = jnp.concatenate(
        [jnp.sum(spread[g * per:(g + 1) * per], axis=0, keepdims=True) for g in range(groups)], axis=0
    )
    g1_copies = fan_row(lambda peer: g1_out, lambda d: g1_in.at[d], g1_s, g1_r)

    part_two = [jnp.zeros((count, BLK), F32) for _ in range(n_row)]
    for b in range(n_blk):
        o = dot_nn(row_lhs[rows_ref[0, b]], split[b])
        term = o[:count, :BLK] + o[count:, :BLK] + o[:count, BLK:]
        place = cols_ref[0, b]
        for q in range(n_row):
            part_two[q] = part_two[q] + (place == q).astype(F32) * term
    for q in range(n_row):
        p2_out[q] = part_two[q]
    p2_copies = fan_row(lambda peer: p2_out.at[peer], lambda d: p2_in.at[d], p2_s, p2_r)

    for copy in g1_copies:
        copy.wait()
    total = g1_out[...]
    for d in range(1, n_row):
        total = total + g1_in[d]
    g2_out[...] = total
    g2_copies = fan_col(lambda peer: g2_out, lambda d: g2_in.at[d], g2_s, g2_r)

    for copy in met_copies:
        copy.wait()
    metric = met_out[...]
    for d in range(1, n_row):
        metric = metric + met_in[d]
    solved = x_own
    for k in range(count):
        ratio = jnp.where(
            sub == k, 0.0,
            jnp.broadcast_to(metric[:, k:k + 1], (count, BLK))
            / jnp.broadcast_to(metric[k:k + 1, k:k + 1], (count, BLK)),
        )
        solved = solved - ratio * solved[k:k + 1]
        metric = metric - ratio * metric[k:k + 1]
    pivots = jnp.sum(jnp.where(lane == sub, metric, 0.0), axis=1, keepdims=True)
    solved = solved / pivots
    high, low = halves(solved)
    y_two = jnp.concatenate(
        [jnp.concatenate([high] * per, axis=0), jnp.concatenate([low] * per, axis=0)], axis=1
    )

    for copy in p2_copies:
        copy.wait()
    image = own_diag + p2_out[my_row]
    for d in range(1, n_row):
        image = image + p2_in[d]
    for copy in p1_copies:
        copy.wait()
    image = image + p1_out[my_col]
    for d in range(1, n_col):
        image = image + p1_in[d]
    image_ref[...] = image

    for copy in g2_copies:
        copy.wait()
    gram = g2_out[...]
    for d in range(1, n_col):
        gram = gram + g2_in[d]
    wide = jnp.concatenate(
        [jnp.broadcast_to(gram[g:g + 1], (per, BLK)) for g in range(groups)], axis=0
    )
    wide = jnp.where(keep, wide, 0.0)
    o = dot_nn(jnp.concatenate(halves(wide), axis=0), y_two)
    resid_ref[...] = image - (o[:count, :BLK] + o[count:, :BLK] + o[:count, BLK:])


def per_device(n_row, n_col, vectors, diag_energy, blocks, block_row, block_col):
    count = vectors.shape[0]
    n_blk = blocks.shape[1]
    groups = count // 8
    piece = (count, BLK)
    vmem = pl.BlockSpec(memory_space=pltpu.VMEM)
    smem = pl.BlockSpec(memory_space=pltpu.SMEM)
    dma = pltpu.SemaphoreType.DMA
    return pl.pallas_call(
        functools.partial(kernel, n_row, n_col),
        out_shape=[jax.ShapeDtypeStruct(piece, F32)] * 2,
        in_specs=[vmem, vmem, smem, smem, pl.BlockSpec(memory_space=pl.ANY)],
        out_specs=[vmem, vmem],
        scratch_shapes=[
            pltpu.VMEM((n_blk, BLK, BLK), F32),
            pltpu.VMEM((n_blk, BLK, 2 * BLK), BF16),
            pltpu.VMEM((n_row,) + piece, F32),
            pltpu.VMEM((n_col,) + piece, F32),
            pltpu.VMEM((n_row, 2 * count, 2 * BLK), BF16),
            pltpu.VMEM((n_col, 2 * count, BLK), BF16),
            pltpu.VMEM(piece, F32),
            pltpu.VMEM((n_row,) + piece, F32),
            pltpu.VMEM((n_col,) + piece, F32),
            pltpu.VMEM((n_col,) + piece, F32),
            pltpu.VMEM((n_row,) + piece, F32),
            pltpu.VMEM((n_row,) + piece, F32),
            pltpu.VMEM((groups, BLK), F32),
            pltpu.VMEM((n_row, groups, BLK), F32),
            pltpu.VMEM((groups, BLK), F32),
            pltpu.VMEM((n_col, groups, BLK), F32),
            dma,
            dma((n_row,)), dma((n_row,)),
            dma((n_col,)), dma((n_col,)),
            dma((n_row,)), dma((n_row,)),
            dma((n_col,)), dma((n_col,)),
            dma((n_row,)), dma((n_row,)),
            dma((n_row,)), dma((n_row,)),
            dma((n_col,)), dma((n_col,)),
        ],
        compiler_params=pltpu.CompilerParams(collective_id=0, has_side_effects=True),
    )(vectors, diag_energy.reshape(1, -1), block_row, block_col, blocks)


def solution(mesh):
    return jax.shard_map(
        functools.partial(per_device, mesh.shape["row"], mesh.shape["col"]),
        mesh=mesh,
        in_specs=(
            P(None, ("row", "col")),
            P(("row", "col")),
            P("row", "col", None, None),
            P("row", "col"),
            P("row", "col"),
        ),
        out_specs=(P(None, ("row", "col")), P(None, ("row", "col"))),
        check_vma=False,
    )
```

```python
import functools

import jax
import jax.numpy as jnp
from jax import lax
from jax.experimental import pallas as pl
from jax.experimental.pallas import tpu as pltpu
from jax.sharding import PartitionSpec as P

BLK = 128
DIRECT = 64
F32 = jnp.float32
BF16 = jnp.bfloat16
MESH = pl.DeviceIdType.MESH


def halves(x):
    high = x.astype(BF16)
    return high, (x - high.astype(F32)).astype(BF16)


def add(terms):
    while len(terms) > 1:
        terms = [a + b for a, b in zip(terms[::2], terms[1::2])] + terms[len(terms) & ~1:]
    return terms[0]


def dot_nt(a, b):
    return lax.dot_general(a, b, (((1,), (1,)), ((), ())), preferred_element_type=F32)


def dot_nn(a, b):
    return lax.dot_general(a, b, (((1,), (0,)), ((), ())), preferred_element_type=F32)


def kernel(
    n_row, n_col,
    x_hbm, diag_hbm, rows_hbm, cols_hbm, blocks_hbm,
    out_ref,
    x_ref, diag_ref, rows_ref, cols_ref, tiles, split, col_x, row_x, col_lhs, row_lhs,
    met_out, met_in, p1_out, p1_in, p2_out, p2_in, g1_out, g1_in, g2_out, g2_in,
    load_sem, cx_s, cx_r, rx_s, rx_r, m_s, m_r, p1_s, p1_r, p2_s, p2_r, g1_s, g1_r, g2_s, g2_r,
):
    count = x_ref.shape[0]
    n_blk = tiles.shape[0]
    my_row = lax.axis_index("row")
    my_col = lax.axis_index("col")

    def fan(axis, size, me, source, target, send, recv):
        copies = []
        for d in range(1, size):
            peer = lax.rem(me + d, size)
            copies.append(
                pltpu.make_async_remote_copy(
                    src_ref=source(peer), dst_ref=target(d), send_sem=send.at[d],
                    recv_sem=recv.at[d], device_id={axis: peer}, device_id_type=MESH,
                )
            )
        for copy in copies:
            copy.start()
        return copies

    fan_row = functools.partial(fan, "row", n_row, my_row)
    fan_col = functools.partial(fan, "col", n_col, my_col)

    x_load, *small_loads, load = [
        pltpu.make_async_copy(source, target, load_sem.at[at])
        for at, (source, target) in enumerate(
            [(x_hbm, x_ref), (diag_hbm, diag_ref), (rows_hbm, rows_ref), (cols_hbm, cols_ref),
             (blocks_hbm.at[0], tiles)]
        )
    ]
    for copy in [x_load, *small_loads, load]:
        copy.start()

    barrier = pltpu.get_barrier_semaphore()
    for d in range(1, n_col):
        pl.semaphore_signal(
            barrier, inc=1, device_id={"col": lax.rem(my_col + d, n_col)}, device_id_type=MESH
        )
    for d in range(1, n_row):
        pl.semaphore_signal(
            barrier, inc=1, device_id={"row": lax.rem(my_row + d, n_row)}, device_id_type=MESH
        )
    x_load.wait()
    pl.semaphore_wait(barrier, n_row + n_col - 2)

    row_copies = fan_col(lambda peer: x_ref, lambda d: row_x.at[my_col], rx_s, rx_r)
    col_copies = fan_row(lambda peer: x_ref, lambda d: col_x.at[my_row], cx_s, cx_r)
    x_own = x_ref[...]
    row_x[my_col] = x_own
    col_x[my_row] = x_own

    for copy in [*small_loads, load]:
        copy.wait()
    for b in range(n_blk):
        high, low = halves(tiles[b])
        split[b] = jnp.concatenate([high, low], axis=1)

    for copy in col_copies:
        copy.wait()
    zero = jnp.zeros((count, BLK), BF16)
    for q in range(n_row):
        high, low = halves(col_x[q])
        col_lhs[q] = jnp.concatenate(
            [jnp.concatenate([high, high], axis=1), jnp.concatenate([low, zero], axis=1)], axis=0
        )
    for copy in row_copies:
        copy.wait()
    row_two = []
    for r in range(n_col):
        high, low = halves(row_x[r])
        both = jnp.concatenate([high, low], axis=0)
        row_lhs[r] = both
        row_two.append(both)

    def fold(o):
        return o[:count, :count] + o[count:, :count] + o[:count, count:]

    x_wide = jnp.concatenate(row_two, axis=1)
    metric_part = fold(dot_nt(x_wide, x_wide))

    part_one = [jnp.zeros((count, BLK), F32) for _ in range(n_col)]
    for b in range(n_blk):
        o = dot_nt(col_lhs[cols_ref[0, b]], split[b])
        term = o[:count] + o[count:]
        place = rows_ref[0, b]
        for r in range(n_col):
            part_one[r] = part_one[r] + (place == r).astype(F32) * term
        if b == n_blk // 4:
            met_out[...] = jnp.concatenate(
                [metric_part, jnp.zeros((count, BLK - count), F32)], axis=1
            )
            met_copies = fan_row(lambda peer: met_out, lambda d: met_in.at[d], m_s, m_r)
    for r in range(n_col):
        p1_out[r] = part_one[r]
    p1_copies = fan_col(lambda peer: p1_out.at[peer], lambda d: p1_in.at[d], p1_s, p1_r)

    own_diag = diag_ref[...] * x_own
    p_two = [jnp.concatenate(halves(p), axis=0) for p in part_one]
    x_two = jnp.concatenate(halves(x_own), axis=0)
    d_two = jnp.concatenate(halves(own_diag), axis=0)
    gram_part = fold(
        dot_nt(
            jnp.concatenate(row_two + p_two + [x_two], axis=1),
            jnp.concatenate(p_two + row_two + [d_two], axis=1),
        )
    )
    per = BLK // count
    groups = count // 8
    lane = lax.broadcasted_iota(jnp.int32, (count, BLK), 1)
    sub = lax.broadcasted_iota(jnp.int32, (count, BLK), 0)
    keep = (lane // count) == (sub % per)
    spread = jnp.where(keep, jnp.concatenate([gram_part] * per, axis=1), 0.0)
    g1_out[...] = jnp.concatenate(
        [jnp.sum(spread[g * per:(g + 1) * per], axis=0, keepdims=True) for g in range(groups)], axis=0
    )
    direct = n_row * n_col <= DIRECT
    if direct:
        g1_copies = []
        for d in range(1, n_row * n_col):
            peer = {"row": lax.rem(my_row + d // n_col, n_row), "col": lax.rem(my_col + d % n_col, n_col)}
            g1_copies.append(
                pltpu.make_async_remote_copy(
                    src_ref=g1_out, dst_ref=g1_in.at[d], send_sem=g1_s.at[d], recv_sem=g1_r.at[d],
                    device_id=peer, device_id_type=MESH,
                )
            )
        for copy in g1_copies:
            copy.start()
    else:
        g1_copies = fan_row(lambda peer: g1_out, lambda d: g1_in.at[d], g1_s, g1_r)

    part_two = [jnp.zeros((count, BLK), F32) for _ in range(n_row)]
    for b in range(n_blk):
        o = dot_nn(row_lhs[rows_ref[0, b]], split[b])
        term = o[:count, :BLK] + o[count:, :BLK] + o[:count, BLK:]
        place = cols_ref[0, b]
        for q in range(n_row):
            part_two[q] = part_two[q] + (place == q).astype(F32) * term
    for q in range(n_row):
        p2_out[q] = part_two[q]
    p2_copies = fan_row(lambda peer: p2_out.at[peer], lambda d: p2_in.at[d], p2_s, p2_r)

    if not direct:
        for copy in g1_copies:
            copy.wait()
        g2_out[...] = add([g1_out[...]] + [g1_in[d] for d in range(1, n_row)])
        g2_copies = fan_col(lambda peer: g2_out, lambda d: g2_in.at[d], g2_s, g2_r)

    for copy in met_copies:
        copy.wait()
    metric = met_out[...]
    for d in range(1, n_row):
        metric = metric + met_in[d]
    solved = x_own
    for k in range(count):
        ratio = jnp.where(
            sub == k, 0.0,
            jnp.broadcast_to(metric[:, k:k + 1], (count, BLK))
            / jnp.broadcast_to(metric[k:k + 1, k:k + 1], (count, BLK)),
        )
        solved = solved - ratio * solved[k:k + 1]
        metric = metric - ratio * metric[k:k + 1]
    pivots = jnp.sum(jnp.where(lane == sub, metric, 0.0), axis=1, keepdims=True)
    solved = solved / pivots
    high, low = halves(solved)
    y_two = jnp.concatenate(
        [jnp.concatenate([high] * per, axis=0), jnp.concatenate([low] * per, axis=0)], axis=1
    )

    for copy in p2_copies:
        copy.wait()
    image = own_diag + p2_out[my_row]
    for d in range(1, n_row):
        image = image + p2_in[d]
    for copy in p1_copies:
        copy.wait()
    image = add([image, p1_out[my_col]] + [p1_in[d] for d in range(1, n_col)])
    out_ref[0] = image

    for copy in g1_copies if direct else g2_copies:
        copy.wait()
    if direct:
        gram = add([g1_out[...]] + [g1_in[d] for d in range(1, n_row * n_col)])
    else:
        gram = add([g2_out[...]] + [g2_in[d] for d in range(1, n_col)])
    wide = jnp.concatenate(
        [jnp.broadcast_to(gram[g:g + 1], (per, BLK)) for g in range(groups)], axis=0
    )
    wide = jnp.where(keep, wide, 0.0)
    o = dot_nn(jnp.concatenate(halves(wide), axis=0), y_two)
    out_ref[1] = image - (o[:count, :BLK] + o[count:, :BLK] + o[:count, BLK:])


def part_kernel(both_ref, image_ref, resid_ref):
    image_ref[...] = both_ref[0]
    resid_ref[...] = both_ref[1]


def per_device(n_row, n_col, vectors, diag_energy, blocks, block_row, block_col):
    count = vectors.shape[0]
    n_blk = blocks.shape[1]
    groups = count // 8
    piece = (count, BLK)
    n_all = n_row * n_col if n_row * n_col <= DIRECT else n_row
    vmem = pl.BlockSpec(memory_space=pltpu.VMEM)
    dma = pltpu.SemaphoreType.DMA
    both = pl.pallas_call(
        functools.partial(kernel, n_row, n_col),
        out_shape=pltpu.VMEM((2,) + piece, F32),
        in_specs=[pl.BlockSpec(memory_space=pl.ANY)] * 5,
        out_specs=vmem,
        scratch_shapes=[
            pltpu.VMEM(piece, F32),
            pltpu.VMEM((1, BLK), F32),
            pltpu.SMEM((1, n_blk), jnp.int32),
            pltpu.SMEM((1, n_blk), jnp.int32),
            pltpu.VMEM((n_blk, BLK, BLK), F32),
            pltpu.VMEM((n_blk, BLK, 2 * BLK), BF16),
            pltpu.VMEM((n_row,) + piece, F32),
            pltpu.VMEM((n_col,) + piece, F32),
            pltpu.VMEM((n_row, 2 * count, 2 * BLK), BF16),
            pltpu.VMEM((n_col, 2 * count, BLK), BF16),
            pltpu.VMEM(piece, F32),
            pltpu.VMEM((n_row,) + piece, F32),
            pltpu.VMEM((n_col,) + piece, F32),
            pltpu.VMEM((n_col,) + piece, F32),
            pltpu.VMEM((n_row,) + piece, F32),
            pltpu.VMEM((n_row,) + piece, F32),
            pltpu.VMEM((groups, BLK), F32),
            pltpu.VMEM((n_all, groups, BLK), F32),
            pltpu.VMEM((groups, BLK), F32),
            pltpu.VMEM((n_col, groups, BLK), F32),
            dma((5,)),
            dma((n_row,)), dma((n_row,)),
            dma((n_col,)), dma((n_col,)),
            dma((n_row,)), dma((n_row,)),
            dma((n_col,)), dma((n_col,)),
            dma((n_row,)), dma((n_row,)),
            dma((n_all,)), dma((n_all,)),
            dma((n_col,)), dma((n_col,)),
        ],
        compiler_params=pltpu.CompilerParams(collective_id=0, has_side_effects=True),
    )(vectors, diag_energy.reshape(1, -1), block_row, block_col, blocks)
    return pl.pallas_call(
        part_kernel,
        out_shape=[jax.ShapeDtypeStruct(piece, F32)] * 2,
        in_specs=[vmem],
        out_specs=[vmem, vmem],
    )(pltpu.with_memory_space_constraint(both, pltpu.VMEM))


def solution(mesh):
    return jax.shard_map(
        functools.partial(per_device, mesh.shape["row"], mesh.shape["col"]),
        mesh=mesh,
        in_specs=(
            P(None, ("row", "col")),
            P(("row", "col")),
            P("row", "col", None, None),
            P("row", "col"),
            P("row", "col"),
        ),
        out_specs=(P(None, ("row", "col")), P(None, ("row", "col"))),
        check_vma=False,
    )
```

```python
import functools

import jax
import jax.numpy as jnp
from jax import lax
from jax.experimental import pallas as pl
from jax.experimental.pallas import tpu as pltpu
from jax.sharding import PartitionSpec as P

BLK = 128
DIRECT = 64
F32 = jnp.float32
BF16 = jnp.bfloat16
MESH = pl.DeviceIdType.MESH


def halves(x):
    high = x.astype(BF16)
    return high, (x - high.astype(F32)).astype(BF16)


def add(terms):
    while len(terms) > 1:
        terms = [a + b for a, b in zip(terms[::2], terms[1::2])] + terms[len(terms) & ~1:]
    return terms[0]


def dot_nt(a, b):
    return lax.dot_general(a, b, (((1,), (1,)), ((), ())), preferred_element_type=F32)


def dot_nn(a, b):
    return lax.dot_general(a, b, (((1,), (0,)), ((), ())), preferred_element_type=F32)


def kernel(
    n_row, n_col,
    x_hbm, diag_hbm, rows_hbm, cols_hbm, blocks_hbm,
    out_ref,
    x_ref, diag_ref, rows_ref, cols_ref, tiles, split, col_x, row_x, col_lhs, row_lhs,
    met_out, met_in, p1_out, p1_in, p2_out, p2_in, g1_out, g1_in, g2_out, g2_in,
    load_sem, cx_s, cx_r, rx_s, rx_r, m_s, m_r, p1_s, p1_r, p2_s, p2_r, g1_s, g1_r, g2_s, g2_r,
):
    count = x_ref.shape[0]
    n_blk = tiles.shape[0]
    my_row = lax.axis_index("row")
    my_col = lax.axis_index("col")

    def fan(axis, size, me, source, target, send, recv):
        copies = []
        for d in range(1, size):
            peer = lax.rem(me + d, size)
            copies.append(
                pltpu.make_async_remote_copy(
                    src_ref=source(peer), dst_ref=target(d), send_sem=send.at[d],
                    recv_sem=recv.at[d], device_id={axis: peer}, device_id_type=MESH,
                )
            )
        for copy in copies:
            copy.start()
        return copies

    fan_row = functools.partial(fan, "row", n_row, my_row)
    fan_col = functools.partial(fan, "col", n_col, my_col)

    x_load, *small_loads, load = [
        pltpu.make_async_copy(source, target, load_sem.at[at])
        for at, (source, target) in enumerate(
            [(x_hbm, x_ref), (diag_hbm, diag_ref), (rows_hbm, rows_ref), (cols_hbm, cols_ref),
             (blocks_hbm.at[0], tiles)]
        )
    ]
    for copy in [x_load, *small_loads, load]:
        copy.start()

    barrier = pltpu.get_barrier_semaphore()
    for d in range(1, n_col):
        pl.semaphore_signal(
            barrier, inc=1, device_id={"col": lax.rem(my_col + d, n_col)}, device_id_type=MESH
        )
    for d in range(1, n_row):
        pl.semaphore_signal(
            barrier, inc=1, device_id={"row": lax.rem(my_row + d, n_row)}, device_id_type=MESH
        )
    x_load.wait()
    pl.semaphore_wait(barrier, n_row + n_col - 2)

    row_copies = fan_col(lambda peer: x_ref, lambda d: row_x.at[my_col], rx_s, rx_r)
    col_copies = fan_row(lambda peer: x_ref, lambda d: col_x.at[my_row], cx_s, cx_r)
    x_own = x_ref[...]
    row_x[my_col] = x_own
    col_x[my_row] = x_own

    for copy in [*small_loads, load]:
        copy.wait()
    for b in range(n_blk):
        high, low = halves(tiles[b])
        split[b] = jnp.concatenate([high, low], axis=1)

    per = BLK // count
    groups = count // 8
    lane = lax.broadcasted_iota(jnp.int32, (count, BLK), 1)
    sub = lax.broadcasted_iota(jnp.int32, (count, BLK), 0)
    keep = (lane // count) == (sub % per)

    def fold(o):
        return o[:count, :count] + o[count:, :count] + o[:count, count:]

    def pack(square):
        spread = jnp.where(keep, jnp.concatenate([square] * per, axis=1), 0.0)
        return jnp.concatenate(
            [jnp.sum(spread[g * per:(g + 1) * per], axis=0, keepdims=True) for g in range(groups)], axis=0
        )

    def unpack(packed):
        wide = jnp.concatenate(
            [jnp.broadcast_to(packed[g:g + 1], (per, BLK)) for g in range(groups)], axis=0
        )
        return jnp.where(keep, wide, 0.0)

    for copy in col_copies:
        copy.wait()
    zero = jnp.zeros((count, BLK), BF16)
    col_two = []
    for q in range(n_row):
        high, low = halves(col_x[q])
        col_lhs[q] = jnp.concatenate(
            [jnp.concatenate([high, high], axis=1), jnp.concatenate([low, zero], axis=1)], axis=0
        )
        col_two.append(jnp.concatenate([high, low], axis=0))
    x_wide = jnp.concatenate(col_two, axis=1)
    met_out[...] = pack(fold(dot_nt(x_wide, x_wide)))
    met_copies = fan_col(lambda peer: met_out, lambda d: met_in.at[d], m_s, m_r)

    part_one = [jnp.zeros((count, BLK), F32) for _ in range(n_col)]
    for b in range(n_blk):
        o = dot_nt(col_lhs[cols_ref[0, b]], split[b])
        term = o[:count] + o[count:]
        place = rows_ref[0, b]
        for r in range(n_col):
            part_one[r] = part_one[r] + (place == r).astype(F32) * term
    for r in range(n_col):
        p1_out[r] = part_one[r]
    p1_copies = fan_col(lambda peer: p1_out.at[peer], lambda d: p1_in.at[d], p1_s, p1_r)

    own_diag = diag_ref[...] * x_own
    p_two = [jnp.concatenate(halves(p), axis=0) for p in part_one]
    x_two = jnp.concatenate(halves(x_own), axis=0)
    d_two = jnp.concatenate(halves(own_diag), axis=0)

    for copy in row_copies:
        copy.wait()
    row_two = []
    for r in range(n_col):
        both = jnp.concatenate(halves(row_x[r]), axis=0)
        row_lhs[r] = both
        row_two.append(both)
    gram_part = fold(
        dot_nt(
            jnp.concatenate(row_two + p_two + [x_two], axis=1),
            jnp.concatenate(p_two + row_two + [d_two], axis=1),
        )
    )
    g1_out[...] = pack(gram_part)
    direct = n_row * n_col <= DIRECT
    if direct:
        g1_copies = []
        for d in range(1, n_row * n_col):
            peer = {"row": lax.rem(my_row + d // n_col, n_row), "col": lax.rem(my_col + d % n_col, n_col)}
            g1_copies.append(
                pltpu.make_async_remote_copy(
                    src_ref=g1_out, dst_ref=g1_in.at[d], send_sem=g1_s.at[d], recv_sem=g1_r.at[d],
                    device_id=peer, device_id_type=MESH,
                )
            )
        for copy in g1_copies:
            copy.start()
    else:
        g1_copies = fan_row(lambda peer: g1_out, lambda d: g1_in.at[d], g1_s, g1_r)

    part_two = [jnp.zeros((count, BLK), F32) for _ in range(n_row)]
    for b in range(n_blk):
        o = dot_nn(row_lhs[rows_ref[0, b]], split[b])
        term = o[:count, :BLK] + o[count:, :BLK] + o[:count, BLK:]
        place = cols_ref[0, b]
        for q in range(n_row):
            part_two[q] = part_two[q] + (place == q).astype(F32) * term
    for q in range(n_row):
        p2_out[q] = part_two[q]
    p2_copies = fan_row(lambda peer: p2_out.at[peer], lambda d: p2_in.at[d], p2_s, p2_r)

    if not direct:
        for copy in g1_copies:
            copy.wait()
        g2_out[...] = add([g1_out[...]] + [g1_in[d] for d in range(1, n_row)])
        g2_copies = fan_col(lambda peer: g2_out, lambda d: g2_in.at[d], g2_s, g2_r)

    for copy in met_copies:
        copy.wait()
    metric = unpack(add([met_out[...]] + [met_in[d] for d in range(1, n_col)]))
    shift = count
    while shift < BLK:
        metric = metric + pltpu.roll(metric, shift, 1)
        shift *= 2
    lines = [jnp.broadcast_to(metric[:, k:k + 1], (count, BLK)) for k in range(count)]
    solved = x_own
    pivots = jnp.ones((count, BLK), F32)
    for k in range(count):
        pivot = lines[k][k:k + 1]
        pivots = jnp.where(sub == k, pivot, pivots)
        ratio = jnp.where(sub == k, 0.0, lines[k] / pivot)
        solved = solved - ratio * solved[k:k + 1]
        for j in range(k + 1, count):
            lines[j] = lines[j] - ratio * lines[j][k:k + 1]
    high, low = halves(solved / pivots)
    y_two = jnp.concatenate(
        [jnp.concatenate([high] * per, axis=0), jnp.concatenate([low] * per, axis=0)], axis=1
    )

    for copy in p2_copies:
        copy.wait()
    image = own_diag + p2_out[my_row]
    for d in range(1, n_row):
        image = image + p2_in[d]
    for copy in p1_copies:
        copy.wait()
    image = add([image, p1_out[my_col]] + [p1_in[d] for d in range(1, n_col)])
    out_ref[0] = image

    for copy in g1_copies if direct else g2_copies:
        copy.wait()
    if direct:
        gram = add([g1_out[...]] + [g1_in[d] for d in range(1, n_row * n_col)])
    else:
        gram = add([g2_out[...]] + [g2_in[d] for d in range(1, n_col)])
    wide = unpack(gram)
    o = dot_nn(jnp.concatenate(halves(wide), axis=0), y_two)
    out_ref[1] = image - (o[:count, :BLK] + o[count:, :BLK] + o[:count, BLK:])


def part_kernel(both_ref, image_ref, resid_ref):
    image_ref[...] = both_ref[0]
    resid_ref[...] = both_ref[1]


def per_device(n_row, n_col, vectors, diag_energy, blocks, block_row, block_col):
    count = vectors.shape[0]
    n_blk = blocks.shape[1]
    groups = count // 8
    piece = (count, BLK)
    n_all = n_row * n_col if n_row * n_col <= DIRECT else n_row
    vmem = pl.BlockSpec(memory_space=pltpu.VMEM)
    dma = pltpu.SemaphoreType.DMA
    both = pl.pallas_call(
        functools.partial(kernel, n_row, n_col),
        out_shape=pltpu.VMEM((2,) + piece, F32),
        in_specs=[pl.BlockSpec(memory_space=pl.ANY)] * 5,
        out_specs=vmem,
        scratch_shapes=[
            pltpu.VMEM(piece, F32),
            pltpu.VMEM((1, BLK), F32),
            pltpu.SMEM((1, n_blk), jnp.int32),
            pltpu.SMEM((1, n_blk), jnp.int32),
            pltpu.VMEM((n_blk, BLK, BLK), F32),
            pltpu.VMEM((n_blk, BLK, 2 * BLK), BF16),
            pltpu.VMEM((n_row,) + piece, F32),
            pltpu.VMEM((n_col,) + piece, F32),
            pltpu.VMEM((n_row, 2 * count, 2 * BLK), BF16),
            pltpu.VMEM((n_col, 2 * count, BLK), BF16),
            pltpu.VMEM((groups, BLK), F32),
            pltpu.VMEM((n_col, groups, BLK), F32),
            pltpu.VMEM((n_col,) + piece, F32),
            pltpu.VMEM((n_col,) + piece, F32),
            pltpu.VMEM((n_row,) + piece, F32),
            pltpu.VMEM((n_row,) + piece, F32),
            pltpu.VMEM((groups, BLK), F32),
            pltpu.VMEM((n_all, groups, BLK), F32),
            pltpu.VMEM((groups, BLK), F32),
            pltpu.VMEM((n_col, groups, BLK), F32),
            dma((5,)),
            dma((n_row,)), dma((n_row,)),
            dma((n_col,)), dma((n_col,)),
            dma((n_col,)), dma((n_col,)),
            dma((n_col,)), dma((n_col,)),
            dma((n_row,)), dma((n_row,)),
            dma((n_all,)), dma((n_all,)),
            dma((n_col,)), dma((n_col,)),
        ],
        compiler_params=pltpu.CompilerParams(collective_id=0, has_side_effects=True),
    )(vectors, diag_energy.reshape(1, -1), block_row, block_col, blocks)
    return pl.pallas_call(
        part_kernel,
        out_shape=[jax.ShapeDtypeStruct(piece, F32)] * 2,
        in_specs=[vmem],
        out_specs=[vmem, vmem],
    )(pltpu.with_memory_space_constraint(both, pltpu.VMEM))


def solution(mesh):
    return jax.shard_map(
        functools.partial(per_device, mesh.shape["row"], mesh.shape["col"]),
        mesh=mesh,
        in_specs=(
            P(None, ("row", "col")),
            P(("row", "col")),
            P("row", "col", None, None),
            P("row", "col"),
            P("row", "col"),
        ),
        out_specs=(P(None, ("row", "col")), P(None, ("row", "col"))),
        check_vma=False,
    )
```

```python
import functools

import jax
import jax.numpy as jnp
from jax import lax
from jax.experimental import pallas as pl
from jax.experimental.pallas import tpu as pltpu
from jax.sharding import PartitionSpec as P

BLK = 128
DIRECT = 64
F32 = jnp.float32
BF16 = jnp.bfloat16
MESH = pl.DeviceIdType.MESH


def halves(x):
    high = x.astype(BF16)
    return high, (x - high.astype(F32)).astype(BF16)


def add(terms):
    while len(terms) > 1:
        terms = [a + b for a, b in zip(terms[::2], terms[1::2])] + terms[len(terms) & ~1:]
    return terms[0]


def dot_nt(a, b):
    return lax.dot_general(a, b, (((1,), (1,)), ((), ())), preferred_element_type=F32)


def dot_nn(a, b):
    return lax.dot_general(a, b, (((1,), (0,)), ((), ())), preferred_element_type=F32)


def kernel(
    n_row, n_col,
    x_hbm, diag_hbm, rows_hbm, cols_hbm, blocks_hbm,
    out_ref,
    x_ref, diag_ref, rows_ref, cols_ref, tiles, split, col_x, row_x, col_lhs, row_lhs,
    met_out, met_in, p1_out, p1_in, p2_out, p2_in, g1_out, g1_in, g2_out, g2_in,
    load_sem, cx_s, cx_r, rx_s, rx_r, m_s, m_r, p1_s, p1_r, p2_s, p2_r, g1_s, g1_r, g2_s, g2_r,
):
    count = x_ref.shape[0]
    n_blk = tiles.shape[0]
    my_row = lax.axis_index("row")
    my_col = lax.axis_index("col")

    def fan(axis, size, me, source, target, send, recv):
        copies = []
        for d in range(1, size):
            peer = lax.rem(me + d, size)
            copies.append(
                pltpu.make_async_remote_copy(
                    src_ref=source(peer), dst_ref=target(d), send_sem=send.at[d],
                    recv_sem=recv.at[d], device_id={axis: peer}, device_id_type=MESH,
                )
            )
        for copy in copies:
            copy.start()
        return copies

    fan_row = functools.partial(fan, "row", n_row, my_row)
    fan_col = functools.partial(fan, "col", n_col, my_col)

    x_load, *small_loads, load = [
        pltpu.make_async_copy(source, target, load_sem.at[at])
        for at, (source, target) in enumerate(
            [(x_hbm, x_ref), (diag_hbm, diag_ref), (rows_hbm, rows_ref), (cols_hbm, cols_ref),
             (blocks_hbm.at[0], tiles)]
        )
    ]
    for copy in [x_load, *small_loads, load]:
        copy.start()

    barrier = pltpu.get_barrier_semaphore()
    for d in range(1, n_col):
        pl.semaphore_signal(
            barrier, inc=1, device_id={"col": lax.rem(my_col + d, n_col)}, device_id_type=MESH
        )
    for d in range(1, n_row):
        pl.semaphore_signal(
            barrier, inc=1, device_id={"row": lax.rem(my_row + d, n_row)}, device_id_type=MESH
        )
    x_load.wait()
    pl.semaphore_wait(barrier, n_row + n_col - 2)

    row_copies = fan_col(lambda peer: x_ref, lambda d: row_x.at[my_col], rx_s, rx_r)
    col_copies = fan_row(lambda peer: x_ref, lambda d: col_x.at[my_row], cx_s, cx_r)
    x_own = x_ref[...]
    row_x[my_col] = x_own
    col_x[my_row] = x_own

    for copy in [*small_loads, load]:
        copy.wait()
    for b in range(n_blk):
        high, low = halves(tiles[b])
        split[b] = jnp.concatenate([high, low], axis=1)

    per = BLK // count
    groups = count // 8
    lane = lax.broadcasted_iota(jnp.int32, (count, BLK), 1)
    sub = lax.broadcasted_iota(jnp.int32, (count, BLK), 0)
    keep = (lane // count) == (sub % per)

    def fold(o):
        return o[:count, :count] + o[count:, :count] + o[:count, count:]

    def pack(square):
        spread = jnp.where(keep, jnp.concatenate([square] * per, axis=1), 0.0)
        return jnp.concatenate(
            [jnp.sum(spread[g * per:(g + 1) * per], axis=0, keepdims=True) for g in range(groups)], axis=0
        )

    def unpack(packed):
        wide = jnp.concatenate(
            [jnp.broadcast_to(packed[g:g + 1], (per, BLK)) for g in range(groups)], axis=0
        )
        return jnp.where(keep, wide, 0.0)

    for copy in col_copies:
        copy.wait()
    zero = jnp.zeros((count, BLK), BF16)
    col_two = []
    for q in range(n_row):
        high, low = halves(col_x[q])
        col_lhs[q] = jnp.concatenate(
            [jnp.concatenate([high, high], axis=1), jnp.concatenate([low, zero], axis=1)], axis=0
        )
        col_two.append(jnp.concatenate([high, low], axis=0))
    x_wide = jnp.concatenate(col_two, axis=1)
    met_out[...] = pack(fold(dot_nt(x_wide, x_wide)))
    met_copies = fan_col(lambda peer: met_out, lambda d: met_in.at[d], m_s, m_r)

    part_one = [jnp.zeros((count, BLK), F32) for _ in range(n_col)]
    for b in range(n_blk):
        o = dot_nt(col_lhs[cols_ref[0, b]], split[b])
        term = o[:count] + o[count:]
        place = rows_ref[0, b]
        for r in range(n_col):
            part_one[r] = part_one[r] + (place == r).astype(F32) * term
    for r in range(n_col):
        p1_out[r] = part_one[r]
    p1_copies = fan_col(lambda peer: p1_out.at[peer], lambda d: p1_in.at[d], p1_s, p1_r)

    own_diag = diag_ref[...] * x_own
    x_two = jnp.concatenate(halves(x_own), axis=0)
    d_two = jnp.concatenate(halves(own_diag), axis=0)

    sum_two = dot_nt(x_two, d_two)

    def take(at, both):
        row_lhs[at] = both
        p_here = jnp.concatenate(halves(p1_out[at]), axis=0)
        return dot_nt(jnp.concatenate([both, p_here], axis=1), jnp.concatenate([p_here, both], axis=1))

    sum_two = sum_two + take(my_col, x_two)
    for d in range(1, n_col):
        row_copies[d - 1].wait()
        at = lax.rem(my_col - d + n_col, n_col)
        sum_two = sum_two + take(at, jnp.concatenate(halves(row_x[at]), axis=0))
    gram_part = fold(sum_two)
    g1_out[...] = pack(gram_part)
    direct = n_row * n_col <= DIRECT
    if direct:
        g1_copies = []
        upper = my_col // (n_col // 2)
        for at in range(1, n_col + 1):
            for over in sorted(range(n_row), key=lambda o: abs(2 * o - n_row)):
                if at == n_col and over == 0:
                    continue
                far = lax.rem(upper * at + (1 - upper) * (n_col - at), n_col)
                slot = over * n_col + far
                peer = {"row": lax.rem(my_row + over, n_row), "col": lax.rem(my_col + far, n_col)}
                g1_copies.append(
                    pltpu.make_async_remote_copy(
                        src_ref=g1_out, dst_ref=g1_in.at[slot], send_sem=g1_s.at[slot],
                        recv_sem=g1_r.at[slot], device_id=peer, device_id_type=MESH,
                    )
                )
        for copy in g1_copies:
            copy.start()
    else:
        g1_copies = fan_row(lambda peer: g1_out, lambda d: g1_in.at[d], g1_s, g1_r)

    part_two = [jnp.zeros((count, BLK), F32) for _ in range(n_row)]
    for b in range(n_blk):
        o = dot_nn(row_lhs[rows_ref[0, b]], split[b])
        term = o[:count, :BLK] + o[count:, :BLK] + o[:count, BLK:]
        place = cols_ref[0, b]
        for q in range(n_row):
            part_two[q] = part_two[q] + (place == q).astype(F32) * term
    for q in range(n_row):
        p2_out[q] = part_two[q]
    p2_copies = fan_row(lambda peer: p2_out.at[peer], lambda d: p2_in.at[d], p2_s, p2_r)

    if not direct:
        for copy in g1_copies:
            copy.wait()
        g2_out[...] = add([g1_out[...]] + [g1_in[d] for d in range(1, n_row)])
        g2_copies = fan_col(lambda peer: g2_out, lambda d: g2_in.at[d], g2_s, g2_r)

    for copy in met_copies:
        copy.wait()
    metric = unpack(add([met_out[...]] + [met_in[d] for d in range(1, n_col)]))
    shift = count
    while shift < BLK:
        metric = metric + pltpu.roll(metric, shift, 1)
        shift *= 2
    lines = [jnp.broadcast_to(metric[:, k:k + 1], (count, BLK)) for k in range(count)]
    solved = x_own
    pivots = jnp.ones((count, BLK), F32)
    for k in range(count):
        pivot = lines[k][k:k + 1]
        pivots = jnp.where(sub == k, pivot, pivots)
        ratio = jnp.where(sub == k, 0.0, lines[k] / pivot)
        solved = solved - ratio * solved[k:k + 1]
        for j in range(k + 1, count):
            lines[j] = lines[j] - ratio * lines[j][k:k + 1]
    high, low = halves(solved / pivots)
    y_two = jnp.concatenate(
        [jnp.concatenate([high] * per, axis=0), jnp.concatenate([low] * per, axis=0)], axis=1
    )

    for copy in p2_copies:
        copy.wait()
    image = own_diag + p2_out[my_row]
    for d in range(1, n_row):
        image = image + p2_in[d]
    for copy in p1_copies:
        copy.wait()
    image = add([image, p1_out[my_col]] + [p1_in[d] for d in range(1, n_col)])
    out_ref[0] = image

    for copy in g1_copies if direct else g2_copies:
        copy.wait()
    if direct:
        gram = add([g1_out[...]] + [g1_in[d] for d in range(1, n_row * n_col)])
    else:
        gram = add([g2_out[...]] + [g2_in[d] for d in range(1, n_col)])
    wide = unpack(gram)
    o = dot_nn(jnp.concatenate(halves(wide), axis=0), y_two)
    out_ref[1] = image - (o[:count, :BLK] + o[count:, :BLK] + o[:count, BLK:])


def part_kernel(both_ref, image_ref, resid_ref):
    image_ref[...] = both_ref[0]
    resid_ref[...] = both_ref[1]


def per_device(n_row, n_col, vectors, diag_energy, blocks, block_row, block_col):
    count = vectors.shape[0]
    n_blk = blocks.shape[1]
    groups = count // 8
    piece = (count, BLK)
    n_all = n_row * n_col if n_row * n_col <= DIRECT else n_row
    vmem = pl.BlockSpec(memory_space=pltpu.VMEM)
    dma = pltpu.SemaphoreType.DMA
    both = pl.pallas_call(
        functools.partial(kernel, n_row, n_col),
        out_shape=pltpu.VMEM((2,) + piece, F32),
        in_specs=[pl.BlockSpec(memory_space=pl.ANY)] * 5,
        out_specs=vmem,
        scratch_shapes=[
            pltpu.VMEM(piece, F32),
            pltpu.VMEM((1, BLK), F32),
            pltpu.SMEM((1, n_blk), jnp.int32),
            pltpu.SMEM((1, n_blk), jnp.int32),
            pltpu.VMEM((n_blk, BLK, BLK), F32),
            pltpu.VMEM((n_blk, BLK, 2 * BLK), BF16),
            pltpu.VMEM((n_row,) + piece, F32),
            pltpu.VMEM((n_col,) + piece, F32),
            pltpu.VMEM((n_row, 2 * count, 2 * BLK), BF16),
            pltpu.VMEM((n_col, 2 * count, BLK), BF16),
            pltpu.VMEM((groups, BLK), F32),
            pltpu.VMEM((n_col, groups, BLK), F32),
            pltpu.VMEM((n_col,) + piece, F32),
            pltpu.VMEM((n_col,) + piece, F32),
            pltpu.VMEM((n_row,) + piece, F32),
            pltpu.VMEM((n_row,) + piece, F32),
            pltpu.VMEM((groups, BLK), F32),
            pltpu.VMEM((n_all, groups, BLK), F32),
            pltpu.VMEM((groups, BLK), F32),
            pltpu.VMEM((n_col, groups, BLK), F32),
            dma((5,)),
            dma((n_row,)), dma((n_row,)),
            dma((n_col,)), dma((n_col,)),
            dma((n_col,)), dma((n_col,)),
            dma((n_col,)), dma((n_col,)),
            dma((n_row,)), dma((n_row,)),
            dma((n_all,)), dma((n_all,)),
            dma((n_col,)), dma((n_col,)),
        ],
        compiler_params=pltpu.CompilerParams(collective_id=0, has_side_effects=True),
    )(vectors, diag_energy.reshape(1, -1), block_row, block_col, blocks)
    return pl.pallas_call(
        part_kernel,
        out_shape=[jax.ShapeDtypeStruct(piece, F32)] * 2,
        in_specs=[vmem],
        out_specs=[vmem, vmem],
    )(pltpu.with_memory_space_constraint(both, pltpu.VMEM))


def solution(mesh):
    return jax.shard_map(
        functools.partial(per_device, mesh.shape["row"], mesh.shape["col"]),
        mesh=mesh,
        in_specs=(
            P(None, ("row", "col")),
            P(("row", "col")),
            P("row", "col", None, None),
            P("row", "col"),
            P("row", "col"),
        ),
        out_specs=(P(None, ("row", "col")), P(None, ("row", "col"))),
        check_vma=False,
    )
```

```python
import functools

import jax
import jax.numpy as jnp
from jax import lax
from jax.experimental import pallas as pl
from jax.experimental.pallas import tpu as pltpu
from jax.sharding import PartitionSpec as P

BLK = 128
DIRECT = 64
F32 = jnp.float32
BF16 = jnp.bfloat16
MESH = pl.DeviceIdType.MESH


def halves(x):
    high = x.astype(BF16)
    return high, (x - high.astype(F32)).astype(BF16)


def add(terms):
    while len(terms) > 1:
        terms = [a + b for a, b in zip(terms[::2], terms[1::2])] + terms[len(terms) & ~1:]
    return terms[0]


def dot_nt(a, b):
    return lax.dot_general(a, b, (((1,), (1,)), ((), ())), preferred_element_type=F32)


def dot_nn(a, b):
    return lax.dot_general(a, b, (((1,), (0,)), ((), ())), preferred_element_type=F32)


def kernel(
    n_row, n_col,
    x_hbm, diag_hbm, rows_hbm, cols_hbm, blocks_hbm,
    out_ref,
    x_ref, diag_ref, rows_ref, cols_ref, tiles, split, col_x, row_x, col_lhs, row_lhs,
    met_out, met_in, p1_out, p1_in, p2_out, p2_in, g1_out, g1_in, g2_out, g2_in,
    load_sem, cx_s, cx_r, rx_s, rx_r, m_s, m_r, p1_s, p1_r, p2_s, p2_r, g1_s, g1_r, g2_s, g2_r,
):
    count = x_ref.shape[0]
    n_blk = tiles.shape[0]
    my_row = lax.axis_index("row")
    my_col = lax.axis_index("col")

    def fan(axis, size, me, source, target, send, recv):
        copies = []
        for d in range(1, size):
            peer = lax.rem(me + d, size)
            copies.append(
                pltpu.make_async_remote_copy(
                    src_ref=source(peer), dst_ref=target(d), send_sem=send.at[d],
                    recv_sem=recv.at[d], device_id={axis: peer}, device_id_type=MESH,
                )
            )
        for copy in copies:
            copy.start()
        return copies

    fan_row = functools.partial(fan, "row", n_row, my_row)
    fan_col = functools.partial(fan, "col", n_col, my_col)

    x_load, *small_loads, load = [
        pltpu.make_async_copy(source, target, load_sem.at[at])
        for at, (source, target) in enumerate(
            [(x_hbm, x_ref), (diag_hbm, diag_ref), (rows_hbm, rows_ref), (cols_hbm, cols_ref),
             (blocks_hbm.at[0], tiles)]
        )
    ]
    for copy in [x_load, *small_loads, load]:
        copy.start()

    barrier = pltpu.get_barrier_semaphore()
    for d in range(1, n_col):
        pl.semaphore_signal(
            barrier, inc=1, device_id={"col": lax.rem(my_col + d, n_col)}, device_id_type=MESH
        )
    for d in range(1, n_row):
        pl.semaphore_signal(
            barrier, inc=1, device_id={"row": lax.rem(my_row + d, n_row)}, device_id_type=MESH
        )
    x_load.wait()
    pl.semaphore_wait(barrier, n_row + n_col - 2)

    upper = my_col // (n_col // 2)
    row_copies = []
    for at in range(1, n_col):
        far = upper * at + (1 - upper) * (n_col - at)
        row_copies.append(
            pltpu.make_async_remote_copy(
                src_ref=x_ref, dst_ref=row_x.at[my_col], send_sem=rx_s.at[far], recv_sem=rx_r.at[far],
                device_id={"col": lax.rem(my_col + far, n_col)}, device_id_type=MESH,
            )
        )
    for copy in row_copies:
        copy.start()
    col_copies = fan_row(lambda peer: x_ref, lambda d: col_x.at[my_row], cx_s, cx_r)
    x_own = x_ref[...]
    row_x[my_col] = x_own
    col_x[my_row] = x_own

    for copy in [*small_loads, load]:
        copy.wait()
    for b in range(n_blk):
        high, low = halves(tiles[b])
        split[b] = jnp.concatenate([high, low], axis=1)

    per = BLK // count
    groups = count // 8
    lane = lax.broadcasted_iota(jnp.int32, (count, BLK), 1)
    sub = lax.broadcasted_iota(jnp.int32, (count, BLK), 0)
    keep = (lane // count) == (sub % per)

    def fold(o):
        return o[:count, :count] + o[count:, :count] + o[:count, count:]

    def pack(square):
        spread = jnp.where(keep, jnp.concatenate([square] * per, axis=1), 0.0)
        return jnp.concatenate(
            [jnp.sum(spread[g * per:(g + 1) * per], axis=0, keepdims=True) for g in range(groups)], axis=0
        )

    def unpack(packed):
        wide = jnp.concatenate(
            [jnp.broadcast_to(packed[g:g + 1], (per, BLK)) for g in range(groups)], axis=0
        )
        return jnp.where(keep, wide, 0.0)

    for copy in col_copies:
        copy.wait()
    zero = jnp.zeros((count, BLK), BF16)
    col_two = []
    for q in range(n_row):
        high, low = halves(col_x[q])
        col_lhs[q] = jnp.concatenate(
            [jnp.concatenate([high, high], axis=1), jnp.concatenate([low, zero], axis=1)], axis=0
        )
        col_two.append(jnp.concatenate([high, low], axis=0))
    x_wide = jnp.concatenate(col_two, axis=1)
    met_out[...] = pack(fold(dot_nt(x_wide, x_wide)))
    met_copies = fan_col(lambda peer: met_out, lambda d: met_in.at[d], m_s, m_r)

    part_one = [jnp.zeros((count, BLK), F32) for _ in range(n_col)]
    for b in range(n_blk):
        o = dot_nt(col_lhs[cols_ref[0, b]], split[b])
        term = o[:count] + o[count:]
        place = rows_ref[0, b]
        for r in range(n_col):
            part_one[r] = part_one[r] + (place == r).astype(F32) * term
    for r in range(n_col):
        p1_out[r] = part_one[r]
    p1_copies = fan_col(lambda peer: p1_out.at[peer], lambda d: p1_in.at[d], p1_s, p1_r)

    own_diag = diag_ref[...] * x_own
    x_two = jnp.concatenate(halves(x_own), axis=0)
    d_two = jnp.concatenate(halves(own_diag), axis=0)

    sum_two = dot_nt(x_two, d_two)

    def take(at, both):
        row_lhs[at] = both
        p_here = jnp.concatenate(halves(p1_out[at]), axis=0)
        return dot_nt(jnp.concatenate([both, p_here], axis=1), jnp.concatenate([p_here, both], axis=1))

    sum_two = sum_two + take(my_col, x_two)
    for copy_at in range(1, n_col):
        row_copies[copy_at - 1].wait()
        far = upper * copy_at + (1 - upper) * (n_col - copy_at)
        at = lax.rem(my_col - far + n_col, n_col)
        sum_two = sum_two + take(at, jnp.concatenate(halves(row_x[at]), axis=0))
    gram_part = fold(sum_two)
    g1_out[...] = pack(gram_part)
    direct = n_row * n_col <= DIRECT
    if direct:
        g1_copies = []
        for at in range(1, n_col + 1):
            for over in sorted(range(n_row), key=lambda o: abs(2 * o - n_row)):
                if at == n_col and over == 0:
                    continue
                far = lax.rem(upper * at + (1 - upper) * (n_col - at), n_col)
                slot = over * n_col + far
                peer = {"row": lax.rem(my_row + over, n_row), "col": lax.rem(my_col + far, n_col)}
                g1_copies.append(
                    pltpu.make_async_remote_copy(
                        src_ref=g1_out, dst_ref=g1_in.at[slot], send_sem=g1_s.at[slot],
                        recv_sem=g1_r.at[slot], device_id=peer, device_id_type=MESH,
                    )
                )
        for copy in g1_copies:
            copy.start()
    else:
        g1_copies = fan_row(lambda peer: g1_out, lambda d: g1_in.at[d], g1_s, g1_r)

    part_two = [jnp.zeros((count, BLK), F32) for _ in range(n_row)]
    for b in range(n_blk):
        o = dot_nn(row_lhs[rows_ref[0, b]], split[b])
        term = o[:count, :BLK] + o[count:, :BLK] + o[:count, BLK:]
        place = cols_ref[0, b]
        for q in range(n_row):
            part_two[q] = part_two[q] + (place == q).astype(F32) * term
    for q in range(n_row):
        p2_out[q] = part_two[q]
    p2_copies = fan_row(lambda peer: p2_out.at[peer], lambda d: p2_in.at[d], p2_s, p2_r)

    if not direct:
        for copy in g1_copies:
            copy.wait()
        g2_out[...] = add([g1_out[...]] + [g1_in[d] for d in range(1, n_row)])
        g2_copies = fan_col(lambda peer: g2_out, lambda d: g2_in.at[d], g2_s, g2_r)

    for copy in met_copies:
        copy.wait()
    metric = unpack(add([met_out[...]] + [met_in[d] for d in range(1, n_col)]))
    shift = count
    while shift < BLK:
        metric = metric + pltpu.roll(metric, shift, 1)
        shift *= 2
    lines = [jnp.broadcast_to(metric[:, k:k + 1], (count, BLK)) for k in range(count)]
    solved = x_own
    pivots = jnp.ones((count, BLK), F32)
    for k in range(count):
        pivot = lines[k][k:k + 1]
        pivots = jnp.where(sub == k, pivot, pivots)
        ratio = jnp.where(sub == k, 0.0, lines[k] / pivot)
        solved = solved - ratio * solved[k:k + 1]
        for j in range(k + 1, count):
            lines[j] = lines[j] - ratio * lines[j][k:k + 1]
    high, low = halves(solved / pivots)
    y_two = jnp.concatenate(
        [jnp.concatenate([high] * per, axis=0), jnp.concatenate([low] * per, axis=0)], axis=1
    )

    for copy in p2_copies:
        copy.wait()
    image = own_diag + p2_out[my_row]
    for d in range(1, n_row):
        image = image + p2_in[d]
    for copy in p1_copies:
        copy.wait()
    image = add([image, p1_out[my_col]] + [p1_in[d] for d in range(1, n_col)])
    out_ref[0] = image

    for copy in g1_copies if direct else g2_copies:
        copy.wait()
    if direct:
        gram = add([g1_out[...]] + [g1_in[d] for d in range(1, n_row * n_col)])
    else:
        gram = add([g2_out[...]] + [g2_in[d] for d in range(1, n_col)])
    wide = unpack(gram)
    o = dot_nn(jnp.concatenate(halves(wide), axis=0), y_two)
    out_ref[1] = image - (o[:count, :BLK] + o[count:, :BLK] + o[:count, BLK:])


def part_kernel(both_ref, image_ref, resid_ref):
    image_ref[...] = both_ref[0]
    resid_ref[...] = both_ref[1]


def per_device(n_row, n_col, vectors, diag_energy, blocks, block_row, block_col):
    count = vectors.shape[0]
    n_blk = blocks.shape[1]
    groups = count // 8
    piece = (count, BLK)
    n_all = n_row * n_col if n_row * n_col <= DIRECT else n_row
    vmem = pl.BlockSpec(memory_space=pltpu.VMEM)
    dma = pltpu.SemaphoreType.DMA
    both = pl.pallas_call(
        functools.partial(kernel, n_row, n_col),
        out_shape=pltpu.VMEM((2,) + piece, F32),
        in_specs=[pl.BlockSpec(memory_space=pl.ANY)] * 5,
        out_specs=vmem,
        scratch_shapes=[
            pltpu.VMEM(piece, F32),
            pltpu.VMEM((1, BLK), F32),
            pltpu.SMEM((1, n_blk), jnp.int32),
            pltpu.SMEM((1, n_blk), jnp.int32),
            pltpu.VMEM((n_blk, BLK, BLK), F32),
            pltpu.VMEM((n_blk, BLK, 2 * BLK), BF16),
            pltpu.VMEM((n_row,) + piece, F32),
            pltpu.VMEM((n_col,) + piece, F32),
            pltpu.VMEM((n_row, 2 * count, 2 * BLK), BF16),
            pltpu.VMEM((n_col, 2 * count, BLK), BF16),
            pltpu.VMEM((groups, BLK), F32),
            pltpu.VMEM((n_col, groups, BLK), F32),
            pltpu.VMEM((n_col,) + piece, F32),
            pltpu.VMEM((n_col,) + piece, F32),
            pltpu.VMEM((n_row,) + piece, F32),
            pltpu.VMEM((n_row,) + piece, F32),
            pltpu.VMEM((groups, BLK), F32),
            pltpu.VMEM((n_all, groups, BLK), F32),
            pltpu.VMEM((groups, BLK), F32),
            pltpu.VMEM((n_col, groups, BLK), F32),
            dma((5,)),
            dma((n_row,)), dma((n_row,)),
            dma((n_col,)), dma((n_col,)),
            dma((n_col,)), dma((n_col,)),
            dma((n_col,)), dma((n_col,)),
            dma((n_row,)), dma((n_row,)),
            dma((n_all,)), dma((n_all,)),
            dma((n_col,)), dma((n_col,)),
        ],
        compiler_params=pltpu.CompilerParams(collective_id=0, has_side_effects=True),
    )(vectors, diag_energy.reshape(1, -1), block_row, block_col, blocks)
    return pl.pallas_call(
        part_kernel,
        out_shape=[jax.ShapeDtypeStruct(piece, F32)] * 2,
        in_specs=[vmem],
        out_specs=[vmem, vmem],
    )(pltpu.with_memory_space_constraint(both, pltpu.VMEM))


def solution(mesh):
    return jax.shard_map(
        functools.partial(per_device, mesh.shape["row"], mesh.shape["col"]),
        mesh=mesh,
        in_specs=(
            P(None, ("row", "col")),
            P(("row", "col")),
            P("row", "col", None, None),
            P("row", "col"),
            P("row", "col"),
        ),
        out_specs=(P(None, ("row", "col")), P(None, ("row", "col"))),
        check_vma=False,
    )
```

```python
import functools

import jax
import jax.numpy as jnp
from jax import lax
from jax.experimental import pallas as pl
from jax.experimental.pallas import tpu as pltpu
from jax.sharding import PartitionSpec as P

BLK = 128
DIRECT = 64
F32 = jnp.float32
BF16 = jnp.bfloat16
MESH = pl.DeviceIdType.MESH


def halves(x):
    high = x.astype(BF16)
    return high, (x - high.astype(F32)).astype(BF16)


def add(terms):
    while len(terms) > 1:
        terms = [a + b for a, b in zip(terms[::2], terms[1::2])] + terms[len(terms) & ~1:]
    return terms[0]


def dot_nt(a, b):
    return lax.dot_general(a, b, (((1,), (1,)), ((), ())), preferred_element_type=F32)


def dot_nn(a, b):
    return lax.dot_general(a, b, (((1,), (0,)), ((), ())), preferred_element_type=F32)


def kernel(
    n_row, n_col,
    x_hbm, diag_hbm, rows_hbm, cols_hbm, blocks_hbm,
    out_ref,
    x_ref, diag_ref, rows_ref, cols_ref, tiles, split, col_x, row_x, col_lhs, row_lhs,
    met_out, met_in, p1_out, p1_in, p2_out, p2_in, g1_out, g1_in, g2_out, g2_in,
    load_sem, cx_s, cx_r, rx_s, rx_r, m_s, m_r, p1_s, p1_r, p2_s, p2_r, g1_s, g1_r, g2_s, g2_r,
):
    count = x_ref.shape[0]
    n_blk = tiles.shape[0]
    my_row = lax.axis_index("row")
    my_col = lax.axis_index("col")

    def fan(axis, size, me, source, target, send, recv):
        copies = []
        for d in range(1, size):
            peer = lax.rem(me + d, size)
            copies.append(
                pltpu.make_async_remote_copy(
                    src_ref=source(peer), dst_ref=target(d), send_sem=send.at[d],
                    recv_sem=recv.at[d], device_id={axis: peer}, device_id_type=MESH,
                )
            )
        for copy in copies:
            copy.start()
        return copies

    fan_row = functools.partial(fan, "row", n_row, my_row)
    fan_col = functools.partial(fan, "col", n_col, my_col)

    barrier = pltpu.get_barrier_semaphore()
    for d in range(1, n_col):
        pl.semaphore_signal(
            barrier, inc=1, device_id={"col": lax.rem(my_col + d, n_col)}, device_id_type=MESH
        )
    for d in range(1, n_row):
        pl.semaphore_signal(
            barrier, inc=1, device_id={"row": lax.rem(my_row + d, n_row)}, device_id_type=MESH
        )

    x_load, *small_loads, load = [
        pltpu.make_async_copy(source, target, load_sem.at[at])
        for at, (source, target) in enumerate(
            [(x_hbm, x_ref), (diag_hbm, diag_ref), (rows_hbm, rows_ref), (cols_hbm, cols_ref),
             (blocks_hbm.at[0], tiles)]
        )
    ]
    for copy in [x_load, *small_loads, load]:
        copy.start()
    x_load.wait()
    pl.semaphore_wait(barrier, n_row + n_col - 2)

    upper = my_col // (n_col // 2)
    row_copies = []
    for at in range(1, n_col):
        far = upper * at + (1 - upper) * (n_col - at)
        row_copies.append(
            pltpu.make_async_remote_copy(
                src_ref=x_ref, dst_ref=row_x.at[my_col], send_sem=rx_s.at[far], recv_sem=rx_r.at[far],
                device_id={"col": lax.rem(my_col + far, n_col)}, device_id_type=MESH,
            )
        )
    for copy in row_copies:
        copy.start()
    col_copies = fan_row(lambda peer: x_ref, lambda d: col_x.at[my_row], cx_s, cx_r)
    x_own = x_ref[...]
    row_x[my_col] = x_own
    col_x[my_row] = x_own

    for copy in [*small_loads, load]:
        copy.wait()
    for b in range(n_blk):
        high, low = halves(tiles[b])
        split[b] = jnp.concatenate([high, low], axis=1)

    per = BLK // count
    groups = count // 8
    lane = lax.broadcasted_iota(jnp.int32, (count, BLK), 1)
    sub = lax.broadcasted_iota(jnp.int32, (count, BLK), 0)
    keep = (lane // count) == (sub % per)

    def fold(o):
        return o[:count, :count] + o[count:, :count] + o[:count, count:]

    def pack(square):
        spread = jnp.where(keep, jnp.concatenate([square] * per, axis=1), 0.0)
        return jnp.concatenate(
            [jnp.sum(spread[g * per:(g + 1) * per], axis=0, keepdims=True) for g in range(groups)], axis=0
        )

    def unpack(packed):
        wide = jnp.concatenate(
            [jnp.broadcast_to(packed[g:g + 1], (per, BLK)) for g in range(groups)], axis=0
        )
        return jnp.where(keep, wide, 0.0)

    for copy in col_copies:
        copy.wait()
    zero = jnp.zeros((count, BLK), BF16)
    col_two = []
    for q in range(n_row):
        high, low = halves(col_x[q])
        col_lhs[q] = jnp.concatenate(
            [jnp.concatenate([high, high], axis=1), jnp.concatenate([low, zero], axis=1)], axis=0
        )
        col_two.append(jnp.concatenate([high, low], axis=0))
    x_wide = jnp.concatenate(col_two, axis=1)
    met_out[...] = pack(fold(dot_nt(x_wide, x_wide)))
    met_copies = fan_col(lambda peer: met_out, lambda d: met_in.at[d], m_s, m_r)

    part_one = [jnp.zeros((count, BLK), F32) for _ in range(n_col)]
    for b in range(n_blk):
        o = dot_nt(col_lhs[cols_ref[0, b]], split[b])
        term = o[:count] + o[count:]
        place = rows_ref[0, b]
        for r in range(n_col):
            part_one[r] = part_one[r] + (place == r).astype(F32) * term
    for r in range(n_col):
        p1_out[r] = part_one[r]
    p1_copies = fan_col(lambda peer: p1_out.at[peer], lambda d: p1_in.at[d], p1_s, p1_r)

    own_diag = diag_ref[...] * x_own
    x_two = jnp.concatenate(halves(x_own), axis=0)
    d_two = jnp.concatenate(halves(own_diag), axis=0)

    sum_two = dot_nt(x_two, d_two)

    def take(at, both):
        row_lhs[at] = both
        p_here = jnp.concatenate(halves(p1_out[at]), axis=0)
        return dot_nt(jnp.concatenate([both, p_here], axis=1), jnp.concatenate([p_here, both], axis=1))

    sum_two = sum_two + take(my_col, x_two)
    for copy_at in range(1, n_col):
        row_copies[copy_at - 1].wait()
        far = upper * copy_at + (1 - upper) * (n_col - copy_at)
        at = lax.rem(my_col - far + n_col, n_col)
        sum_two = sum_two + take(at, jnp.concatenate(halves(row_x[at]), axis=0))
    gram_part = fold(sum_two)
    g1_out[...] = pack(gram_part)
    direct = n_row * n_col <= DIRECT
    if direct:
        g1_copies = []
        for at in range(1, n_col + 1):
            for over in sorted(range(n_row), key=lambda o: abs(2 * o - n_row)):
                if at == n_col and over == 0:
                    continue
                far = lax.rem(upper * at + (1 - upper) * (n_col - at), n_col)
                slot = over * n_col + far
                peer = {"row": lax.rem(my_row + over, n_row), "col": lax.rem(my_col + far, n_col)}
                g1_copies.append(
                    pltpu.make_async_remote_copy(
                        src_ref=g1_out, dst_ref=g1_in.at[slot], send_sem=g1_s.at[slot],
                        recv_sem=g1_r.at[slot], device_id=peer, device_id_type=MESH,
                    )
                )
        for copy in g1_copies:
            copy.start()
    else:
        g1_copies = fan_row(lambda peer: g1_out, lambda d: g1_in.at[d], g1_s, g1_r)

    part_two = [jnp.zeros((count, BLK), F32) for _ in range(n_row)]
    for b in range(n_blk):
        o = dot_nn(row_lhs[rows_ref[0, b]], split[b])
        term = o[:count, :BLK] + o[count:, :BLK] + o[:count, BLK:]
        place = cols_ref[0, b]
        for q in range(n_row):
            part_two[q] = part_two[q] + (place == q).astype(F32) * term
    for q in range(n_row):
        p2_out[q] = part_two[q]
    p2_copies = fan_row(lambda peer: p2_out.at[peer], lambda d: p2_in.at[d], p2_s, p2_r)

    if not direct:
        for copy in g1_copies:
            copy.wait()
        g2_out[...] = add([g1_out[...]] + [g1_in[d] for d in range(1, n_row)])
        g2_copies = fan_col(lambda peer: g2_out, lambda d: g2_in.at[d], g2_s, g2_r)

    for copy in met_copies:
        copy.wait()
    metric = unpack(add([met_out[...]] + [met_in[d] for d in range(1, n_col)]))
    shift = count
    while shift < BLK:
        metric = metric + pltpu.roll(metric, shift, 1)
        shift *= 2
    lines = [jnp.broadcast_to(metric[:, k:k + 1], (count, BLK)) for k in range(count)]
    solved = x_own
    pivots = jnp.ones((count, BLK), F32)
    for k in range(count):
        pivot = lines[k][k:k + 1]
        pivots = jnp.where(sub == k, pivot, pivots)
        ratio = jnp.where(sub == k, 0.0, lines[k] / pivot)
        solved = solved - ratio * solved[k:k + 1]
        for j in range(k + 1, count):
            lines[j] = lines[j] - ratio * lines[j][k:k + 1]
    high, low = halves(solved / pivots)
    y_two = jnp.concatenate(
        [jnp.concatenate([high] * per, axis=0), jnp.concatenate([low] * per, axis=0)], axis=1
    )

    for copy in p2_copies:
        copy.wait()
    image = own_diag + p2_out[my_row]
    for d in range(1, n_row):
        image = image + p2_in[d]
    for copy in p1_copies:
        copy.wait()
    image = add([image, p1_out[my_col]] + [p1_in[d] for d in range(1, n_col)])
    out_ref[0] = image

    for copy in g1_copies if direct else g2_copies:
        copy.wait()
    if direct:
        gram = add([g1_out[...]] + [g1_in[d] for d in range(1, n_row * n_col)])
    else:
        gram = add([g2_out[...]] + [g2_in[d] for d in range(1, n_col)])
    wide = unpack(gram)
    o = dot_nn(jnp.concatenate(halves(wide), axis=0), y_two)
    out_ref[1] = image - (o[:count, :BLK] + o[count:, :BLK] + o[:count, BLK:])


def part_kernel(both_ref, image_ref, resid_ref):
    image_ref[...] = both_ref[0]
    resid_ref[...] = both_ref[1]


def per_device(n_row, n_col, vectors, diag_energy, blocks, block_row, block_col):
    count = vectors.shape[0]
    n_blk = blocks.shape[1]
    groups = count // 8
    piece = (count, BLK)
    n_all = n_row * n_col if n_row * n_col <= DIRECT else n_row
    vmem = pl.BlockSpec(memory_space=pltpu.VMEM)
    dma = pltpu.SemaphoreType.DMA
    both = pl.pallas_call(
        functools.partial(kernel, n_row, n_col),
        out_shape=pltpu.VMEM((2,) + piece, F32),
        in_specs=[pl.BlockSpec(memory_space=pl.ANY)] * 5,
        out_specs=vmem,
        scratch_shapes=[
            pltpu.VMEM(piece, F32),
            pltpu.VMEM((1, BLK), F32),
            pltpu.SMEM((1, n_blk), jnp.int32),
            pltpu.SMEM((1, n_blk), jnp.int32),
            pltpu.VMEM((n_blk, BLK, BLK), F32),
            pltpu.VMEM((n_blk, BLK, 2 * BLK), BF16),
            pltpu.VMEM((n_row,) + piece, F32),
            pltpu.VMEM((n_col,) + piece, F32),
            pltpu.VMEM((n_row, 2 * count, 2 * BLK), BF16),
            pltpu.VMEM((n_col, 2 * count, BLK), BF16),
            pltpu.VMEM((groups, BLK), F32),
            pltpu.VMEM((n_col, groups, BLK), F32),
            pltpu.VMEM((n_col,) + piece, F32),
            pltpu.VMEM((n_col,) + piece, F32),
            pltpu.VMEM((n_row,) + piece, F32),
            pltpu.VMEM((n_row,) + piece, F32),
            pltpu.VMEM((groups, BLK), F32),
            pltpu.VMEM((n_all, groups, BLK), F32),
            pltpu.VMEM((groups, BLK), F32),
            pltpu.VMEM((n_col, groups, BLK), F32),
            dma((5,)),
            dma((n_row,)), dma((n_row,)),
            dma((n_col,)), dma((n_col,)),
            dma((n_col,)), dma((n_col,)),
            dma((n_col,)), dma((n_col,)),
            dma((n_row,)), dma((n_row,)),
            dma((n_all,)), dma((n_all,)),
            dma((n_col,)), dma((n_col,)),
        ],
        compiler_params=pltpu.CompilerParams(collective_id=0, has_side_effects=True),
    )(vectors, diag_energy.reshape(1, -1), block_row, block_col, blocks)
    return pl.pallas_call(
        part_kernel,
        out_shape=[jax.ShapeDtypeStruct(piece, F32)] * 2,
        in_specs=[vmem],
        out_specs=[vmem, vmem],
    )(pltpu.with_memory_space_constraint(both, pltpu.VMEM))


def solution(mesh):
    return jax.shard_map(
        functools.partial(per_device, mesh.shape["row"], mesh.shape["col"]),
        mesh=mesh,
        in_specs=(
            P(None, ("row", "col")),
            P(("row", "col")),
            P("row", "col", None, None),
            P("row", "col"),
            P("row", "col"),
        ),
        out_specs=(P(None, ("row", "col")), P(None, ("row", "col"))),
        check_vma=False,
    )
```
